256 devices in a mesh: bubble: 16 (over y_hi, z), panel: 16 (over y_lo, x, core).
Axes of the slice: x: 4, y: 4 (y_hi: 2, y_lo: 2; y = y_hi * 2 + y_lo), z: 8, core: 2. Of those that a mesh axis runs over, the one named last changes fastest.
Arguments:
- density: float32 [128, 12288], P('bubble', 'panel'), may hold values from -6 to 6
- right_side: float32 [128, 12288], P('bubble', 'panel'), may hold values from -6 to 6
- inv_diag: bfloat16 [128, 96, 128, 128], P('bubble', 'panel')
- near_vals: bfloat16 [128, 96, 4, 128, 128], P('bubble', 'panel'), may hold values from -0.25 to 0.25
- near_bubble: int32 [128, 96, 4], P('bubble', 'panel'), may hold values from 0 to 127, as said below
- near_block: int32 [128, 96, 4], P('bubble', 'panel'), may hold values from 0 to 95
- near_count: int32 [128, 96], P('bubble', 'panel'), may hold values from 1 to 4, as said below
- colour: int32 [128], P('bubble'), may hold values from 0 to 1
- moment_map: bfloat16 [128, 16, 12288], P('bubble', None, 'panel'), may hold values from -0.0546875 to 0.0546875
- spread_map: bfloat16 [128, 16, 12288], P('bubble', None, 'panel'), may hold values from -0.125 to 0.125
- centres: float32 [3, 128], replicated, may hold values from 0.2 to 6
Outputs:
- relaxed: float32 [128, 12288], P('bubble', 'panel')
The draws below stay inside these ranges and needn't reach their ends.
Inputs may be any that keep to these rules, and one draw needn't show every extreme that they name: `near_bubble`: every slot of bubble b names a bubble within 8 of b. `near_count`: the first row block of every bubble uses all 4 slots.
All inputs are finite; a program needn't handle non-finite values.
Results may differ from the reference program's by a relative error of at most 0.0041.
Values may be sent and summed in bfloat16 or wider, within the bound.
No kernel may reach another device: no remote copies, remote signals or barrier semaphores. Data moves between devices by JAX's collectives and lax.ppermute only.
A program may use at most 64 MiB of HBM per device.

```python
import jax
import jax.numpy as jnp
from jax import lax

P_SIZE = 12288
BLK = 128
K = 16
SLOTS = 4
BUB_DEV = 8
BUBBLES = 128
NB = 96


def draw_inv_diag(key, part):
    shape = (BUBBLES, P_SIZE // BLK, BLK, BLK)
    spread = jax.random.normal(key, shape, jnp.float32) * (0.5 / BLK ** 0.5)
    rows = lax_iota_rows(shape)
    return (spread + rows).astype(jnp.bfloat16)


def lax_iota_rows(shape):
    left = jnp.arange(shape[2])[:, None]
    right = jnp.arange(shape[3])[None, :]
    return jnp.broadcast_to((left == right).astype(jnp.float32), shape)


def draw_near_bubble(key, part):
    shape = (BUBBLES, P_SIZE // BLK, SLOTS)
    offsets = jax.random.randint(key, shape, -BUB_DEV, BUB_DEV + 1)
    owners = jnp.arange(BUBBLES, dtype=jnp.int32)[:, None, None]
    return jnp.clip(owners + offsets, 0, BUBBLES - 1).astype(jnp.int32)


def draw_near_count(key, part):
    counts = jax.random.randint(key, (BUBBLES, P_SIZE // BLK), 1, SLOTS + 1)
    return counts.at[:, 0].set(SLOTS).astype(jnp.int32)


def with_ends(array, key, smallest, largest):
    longest = array.shape.index(max(array.shape))
    spots = []
    for shift in (0, 1):
        where = [jax.random.randint(jax.random.fold_in(key, axis), (), 0, length) for axis, length in enumerate(array.shape)]
        where[longest] = (where[longest] + shift) % array.shape[longest]
        spots.append(tuple(where))
    return array.at[spots[0]].set(smallest).at[spots[1]].set(largest)


def shard_levels(own_key, shape, pieces, low, high):
    loudness, own = 1.0, jax.random.fold_in(own_key, 6)
    for position, parts in pieces:
        steps = jnp.exp(jax.random.uniform(jax.random.fold_in(own, position), (parts,), jnp.float32, low / len(pieces), high / len(pieces)))
        loudness = loudness * jnp.repeat(steps, shape[position] // parts).reshape([-1 if axis == position else 1 for axis in range(len(shape))])
    return loudness


def scatter_about(own_key, extent, scale, bound, split=(), kind=jnp.bfloat16):
    gain = shard_levels(own_key, extent, split, -0.22, 0.18) if split else 1.0
    values = jax.random.normal(own_key, extent, jnp.float32) * scale * gain
    return jnp.minimum(jnp.maximum(values, -bound), bound).astype(kind)


def setup_inputs(seed: int = 0) -> dict:
    streams_of = jax.random.split(jax.random.key(seed), 12)
    density = scatter_about(streams_of[0], (BUBBLES, P_SIZE), 1.0, 6.0, ((0, 16), (1, 16)), jnp.float32)
    right_side = scatter_about(streams_of[1], (BUBBLES, P_SIZE), 1.0, 6.0, ((0, 16), (1, 16)), jnp.float32)
    inv_diag = draw_inv_diag(jax.random.fold_in(streams_of[11], 71), 0)
    near_vals = scatter_about(streams_of[3], (BUBBLES, NB, SLOTS, BLK, BLK), (BLK * SLOTS) ** -0.5, 0.25, ((0, 16), (1, 16)))
    near_bubble = draw_near_bubble(jax.random.fold_in(streams_of[11], 71), 0)
    near_block = with_ends(jax.random.randint(streams_of[5], (BUBBLES, NB, SLOTS), 0, NB), jax.random.fold_in(streams_of[5], 1), 0, NB - 1).astype(jnp.int32)
    near_count = draw_near_count(jax.random.fold_in(streams_of[11], 71), 0)
    colour = with_ends(jax.random.randint(streams_of[7], (BUBBLES,), 0, 2), jax.random.fold_in(streams_of[7], 1), 0, 1).astype(jnp.int32)
    moment_map = scatter_about(streams_of[8], (BUBBLES, K, P_SIZE), P_SIZE ** -0.5, 0.0546875, ((0, 16), (2, 16)))
    spread_map = scatter_about(streams_of[9], (BUBBLES, K, P_SIZE), (K * BUBBLES) ** -0.5, 0.125, ((0, 16), (2, 16)))
    centres = jnp.clip(jax.random.uniform(streams_of[10], (3, BUBBLES), jnp.float32, 0.2, 6.0), 0.2, 6.0)
    return dict(density=density, right_side=right_side, inv_diag=inv_diag, near_vals=near_vals, near_bubble=near_bubble, near_block=near_block, near_count=near_count, colour=colour, moment_map=moment_map, spread_map=spread_map, centres=centres)


def near_field(dens_bf, near_vals, near_bubble, near_block, near_count):
    blocks = dens_bf.reshape(BUBBLES, P_SIZE // BLK, BLK)

    def one_bubble(items):
        block_vals, src_bubble, src_block, counts = items
        sources = blocks[src_bubble, src_block]
        live_slot = jnp.arange(SLOTS)[None, :] < counts[:, None]
        sources = jnp.where(live_slot[:, :, None], sources, jnp.zeros_like(sources))
        return jnp.einsum('rsij,rsj->ri', block_vals.astype(jnp.float32), sources.astype(jnp.float32))
    return lax.map(one_bubble, (near_vals, near_bubble, near_block, near_count))

def far_kernel(centres):
    diff = centres[:, :, None] - centres[:, None, :]
    direct_sq = lax.optimization_barrier(jnp.sum(diff * diff, axis=0))
    mirrored = centres[2][:, None] + centres[2][None, :]
    image_sq = diff[0] * diff[0] + diff[1] * diff[1] + mirrored * mirrored
    kernel = 1.0 / jnp.sqrt(direct_sq + 1.0) + 1.0 / jnp.sqrt(image_sq + 1.0)
    gap = jnp.abs(jnp.arange(BUBBLES)[:, None] - jnp.arange(BUBBLES)[None, :])
    return jnp.where(gap > BUB_DEV, kernel, jnp.zeros_like(kernel))

def reference(density, right_side, inv_diag, near_vals, near_bubble, near_block, near_count, colour, moment_map, spread_map, centres):
    kernel = far_kernel(centres)
    relaxed = density
    for colour_now in range(2):
        dens_bf = relaxed.astype(jnp.bfloat16)
        near = near_field(dens_bf, near_vals, near_bubble, near_block, near_count).reshape(BUBBLES, P_SIZE)
        moments = jnp.einsum('bki,bi->bk', moment_map.astype(jnp.float32), dens_bf.astype(jnp.float32))
        far_coeff = jnp.dot(kernel, moments, precision=lax.Precision.HIGHEST).astype(jnp.bfloat16)
        far = jnp.einsum('bki,bk->bi', spread_map.astype(jnp.float32), far_coeff.astype(jnp.float32))
        remainder = (right_side - near - far).astype(jnp.bfloat16).reshape(BUBBLES, P_SIZE // BLK, BLK)

        def solve_one(items):
            inverse, rest_rows = items
            return jnp.einsum('rij,rj->ri', inverse.astype(jnp.float32), rest_rows.astype(jnp.float32))
        updated = lax.map(solve_one, (inv_diag, remainder)).reshape(BUBBLES, P_SIZE)
        relaxed = jnp.where((colour == colour_now)[:, None], updated, relaxed)
    return relaxed
```

```python
import functools

import jax
import jax.numpy as jnp
from jax import lax
from jax.experimental import pallas as pl
from jax.experimental.pallas import tpu as pltpu
from jax.sharding import PartitionSpec as P

NT = (((1,), (1,)), ((), ()))
NN = (((1,), (0,)), ((), ()))


def row_ids(shape):
    return lax.broadcasted_iota(jnp.int32, shape, 0)


def emit_message(tiles, moment_map, message):
    bub, lanes = tiles[0].shape
    peers, slots = message.shape[:2]
    k = lanes // bub
    dens = jnp.concatenate(tiles, axis=1).astype(jnp.bfloat16)
    cross = lax.dot_general(dens, moment_map[...], NT, preferred_element_type=jnp.float32)
    rows = row_ids((bub, lanes))
    own = lax.broadcasted_iota(jnp.int32, (bub, lanes), 1) // k == rows
    share = jnp.sum(jnp.where(own, cross, 0.0), axis=0, keepdims=True)
    top = share.astype(jnp.bfloat16).astype(jnp.float32)
    rest = share - top
    mid = rest.astype(jnp.bfloat16).astype(jnp.float32)
    low = rest - mid
    parts = jnp.where(
        rows == 0, top, jnp.where(rows == 1, mid, jnp.where(rows == 2, low, 0.0))
    ).astype(jnp.bfloat16)
    blocks = [t.astype(jnp.bfloat16) for t in tiles] + [parts]
    for p in range(peers):
        for j in range(slots):
            message[p, j] = blocks[j]


def first_kernel(density, moment_map, message):
    n = message.shape[1] - 1
    w = message.shape[3]
    tiles = [density[:, j * w : (j + 1) * w] for j in range(n)]
    emit_message(tiles, moment_map, message)


def moment_kernel(received, out):
    peers, slots = received.shape[:2]
    total = received[0, slots - 1].astype(jnp.float32)
    for p in range(1, peers):
        total = total + received[p, slots - 1].astype(jnp.float32)
    row = jnp.sum(total, axis=0, keepdims=True)
    for g in range(out.shape[0]):
        out[g] = row


def sweep_kernel(
    colour_now,
    last,
    index,
    colour,
    before,
    own,
    after,
    moments,
    far_weight,
    spread_map,
    right_side,
    relaxed,
    moment_map,
    near_vals,
    inv_diag,
    *refs,
):
    if last:
        out, sources, vals, invs, acc, sem_v, sem_i = refs
    else:
        out, message, sources, vals, invs, acc, sem_v, sem_i = refs
    bub, nblk, slots, blk, _ = near_vals.shape
    peers = own.shape[0]
    k = blk // bub

    def copy_v(b):
        return pltpu.make_async_copy(near_vals.at[b], vals.at[b], sem_v.at[b])

    def copy_i(b):
        return pltpu.make_async_copy(inv_diag.at[b], invs.at[b], sem_i.at[b])

    for b in range(bub):

        @pl.when(colour[b] == colour_now)
        def _():
            copy_v(b).start()

    for b in range(bub):

        @pl.when(colour[b] == colour_now)
        def _():
            copy_i(b).start()

    rows = row_ids((bub, blk))
    for o, ref in enumerate((before, own, after)):
        for p in range(peers):
            for j in range(nblk):
                at = ((o * peers + p) * nblk + j) * bub
                sources[at : at + bub, :] = ref[p, j].astype(jnp.float32)
    sources[3 * peers * nblk * bub :, :] = jnp.zeros((bub, blk), jnp.float32)
    acc[...] = jnp.zeros_like(acc)

    g = far_weight[0] * moments[0]
    for q in range(1, moments.shape[0]):
        g = g + far_weight[q] * moments[q]
    shift = blk // 2
    while shift >= k:
        g = g + pltpu.roll(g, shift, 1)
        shift //= 2
    mine = lax.broadcasted_iota(jnp.int32, (bub, blk), 1) // k == rows
    coeff = jnp.where(mine, g, 0.0).astype(jnp.bfloat16)
    far = lax.dot_general(coeff, spread_map[...], NN, preferred_element_type=jnp.float32)

    def near_of(b, carry):
        @pl.when(colour[b] == colour_now)
        def _():
            copy_v(b).wait()
            here = rows == b
            for r in range(nblk):
                total = acc[r]
                for s in range(slots):
                    i = index[(b * nblk + r) * slots + s]
                    src = jnp.where(here, sources[pl.ds(i, 1), :], 0.0).astype(jnp.bfloat16)
                    total = total + lax.dot_general(
                        src, vals[b, r, s], NT, preferred_element_type=jnp.float32
                    )
                acc[r] = total

        return carry

    lax.fori_loop(0, bub, near_of, 0)
    for r in range(nblk):
        cols = slice(r * blk, (r + 1) * blk)
        acc[r] = right_side[:, cols] - acc[r] - far[:, cols]
        out[:, cols] = jnp.zeros((bub, blk), jnp.float32)

    def solve(b, carry):
        @pl.when(colour[b] == colour_now)
        def _():
            copy_i(b).wait()
            here = rows == b
            for r in range(nblk):
                cols = slice(r * blk, (r + 1) * blk)
                rest = jnp.where(here, acc[r], 0.0).astype(jnp.bfloat16)
                out[:, cols] += lax.dot_general(
                    rest, invs[b, r], NT, preferred_element_type=jnp.float32
                )

        return carry

    lax.fori_loop(0, bub, solve, 0)
    colours = jnp.zeros((bub, blk), jnp.int32)
    for b in range(bub):
        colours = jnp.where(rows == b, colour[b], colours)
    live = colours == colour_now
    tiles = []
    for r in range(nblk):
        cols = slice(r * blk, (r + 1) * blk)
        tile = jnp.where(live, out[:, cols], relaxed[:, cols])
        out[:, cols] = tile
        tiles.append(tile)
    if not last:
        emit_message(tiles, moment_map, message)


def far_weights(centres, my_bubbles, reach, k):
    n_bub, total = my_bubbles.shape[0], centres.shape[1]
    groups = total // n_bub
    theirs = jnp.repeat(centres, k, axis=1).reshape(3, groups, 1, n_bub * k)
    mine = centres[:, my_bubbles].reshape(3, 1, n_bub, 1)
    diff = mine - theirs
    direct_sq = diff[0] * diff[0] + diff[1] * diff[1] + diff[2] * diff[2]
    mirrored = mine[2] + theirs[2]
    image_sq = diff[0] * diff[0] + diff[1] * diff[1] + mirrored * mirrored
    kernel = 1.0 / jnp.sqrt(direct_sq + 1.0) + 1.0 / jnp.sqrt(image_sq + 1.0)
    lane = lax.broadcasted_iota(jnp.int32, kernel.shape, 2)
    q = lax.broadcasted_iota(jnp.int32, kernel.shape, 0) * n_bub + lane // k
    gap = jnp.abs(my_bubbles.reshape(1, n_bub, 1) - q)
    return jnp.where(gap > reach, kernel, jnp.zeros_like(kernel))


VMEM = pl.BlockSpec(memory_space=pltpu.VMEM)
SMEM = pl.BlockSpec(memory_space=pltpu.SMEM)
ANY = pl.BlockSpec(memory_space=pl.ANY)


def per_device(
    density,
    right_side,
    inv_diag,
    near_vals,
    near_bubble,
    near_block,
    near_count,
    colour,
    moment_map,
    spread_map,
    centres,
):
    bub, nblk, slots, blk, _ = near_vals.shape
    k = moment_map.shape[1]
    panels = nblk * blk
    peers, groups = lax.axis_size("panel"), lax.axis_size("bubble")
    my_index = lax.axis_index("bubble")
    my_bubbles = my_index * bub + jnp.arange(bub, dtype=jnp.int32)
    far_weight = far_weights(centres, my_bubbles, bub, k)
    moment_map = moment_map.reshape(bub * k, panels)
    spread_map = spread_map.reshape(bub * k, panels)

    local = near_bubble - (my_index * bub - bub)
    row = ((local // bub) * peers * nblk + near_block) * bub + local % bub
    live = jnp.arange(slots)[None, None, :] < near_count[:, :, None]
    index = jnp.where(live, row, 3 * peers * nblk * bub).reshape(-1)

    message_shape = jax.ShapeDtypeStruct((peers, nblk + 1, bub, blk), jnp.bfloat16)
    relaxed_shape = jax.ShapeDtypeStruct((bub, panels), jnp.float32)
    up = [(i, (i + 1) % groups) for i in range(groups)]
    down = [(j, i) for i, j in up]

    message = pl.pallas_call(
        first_kernel, out_shape=message_shape, in_specs=[VMEM, VMEM], out_specs=VMEM, name="first"
    )(density, moment_map)
    relaxed = density
    for colour_now in range(2):
        last = colour_now == 1
        received = lax.all_to_all(message, "panel", 0, 0, tiled=True)
        before = lax.ppermute(received, "bubble", up)
        after = lax.ppermute(received, "bubble", down)
        own_moments = pl.pallas_call(
            moment_kernel,
            out_shape=jax.ShapeDtypeStruct((groups, 1, blk), jnp.float32),
            in_specs=[VMEM],
            out_specs=VMEM,
            name="moments",
        )(received)
        moments = lax.all_to_all(own_moments, "bubble", 0, 0, tiled=True)
        outs = pl.pallas_call(
            functools.partial(sweep_kernel, colour_now, last),
            out_shape=[relaxed_shape] if last else [relaxed_shape, message_shape],
            in_specs=[SMEM, SMEM] + [VMEM] * 9 + [ANY, ANY],
            out_specs=[VMEM] if last else [VMEM, VMEM],
            scratch_shapes=[
                pltpu.VMEM(((3 * peers * nblk + 1) * bub, blk), jnp.float32),
                pltpu.VMEM((bub, nblk, slots, blk, blk), jnp.bfloat16),
                pltpu.VMEM((bub, nblk, blk, blk), jnp.bfloat16),
                pltpu.VMEM((nblk, bub, blk), jnp.float32),
                pltpu.SemaphoreType.DMA((bub,)),
                pltpu.SemaphoreType.DMA((bub,)),
            ],
            name=f"sweep{colour_now}",
        )(
            index,
            colour,
            before,
            received,
            after,
            moments,
            far_weight,
            spread_map,
            right_side,
            relaxed,
            moment_map,
            near_vals,
            inv_diag,
        )
        if last:
            (relaxed,) = outs
        else:
            relaxed, message = outs
    return relaxed


def solution(mesh):
    in_specs = (
        P("bubble", "panel"),
        P("bubble", "panel"),
        P("bubble", "panel", None, None),
        P("bubble", "panel", None, None, None),
        P("bubble", "panel", None),
        P("bubble", "panel", None),
        P("bubble", "panel"),
        P("bubble"),
        P("bubble", None, "panel"),
        P("bubble", None, "panel"),
        P(),
    )
    out_specs = P("bubble", "panel")
    return jax.shard_map(
        per_device, mesh=mesh, in_specs=in_specs, out_specs=out_specs, check_vma=False
    )
```

```python
import functools

import jax
import jax.numpy as jnp
from jax import lax
from jax.experimental import pallas as pl
from jax.experimental.pallas import tpu as pltpu
from jax.sharding import PartitionSpec as P

NT = (((1,), (1,)), ((), ()))
NN = (((1,), (0,)), ((), ()))


def row_ids(shape):
    return lax.broadcasted_iota(jnp.int32, shape, 0)


def emit_message(tiles, moment_map, message):
    bub, lanes = tiles[0].shape
    peers, slots = message.shape[:2]
    k = lanes // bub
    dens = jnp.concatenate(tiles, axis=1).astype(jnp.bfloat16)
    cross = lax.dot_general(dens, moment_map[...], NT, preferred_element_type=jnp.float32)
    rows = row_ids((bub, lanes))
    own = lax.broadcasted_iota(jnp.int32, (bub, lanes), 1) // k == rows
    share = jnp.sum(jnp.where(own, cross, 0.0), axis=0, keepdims=True)
    top = share.astype(jnp.bfloat16).astype(jnp.float32)
    rest = share - top
    mid = rest.astype(jnp.bfloat16).astype(jnp.float32)
    low = rest - mid
    parts = jnp.where(
        rows == 0, top, jnp.where(rows == 1, mid, jnp.where(rows == 2, low, 0.0))
    ).astype(jnp.bfloat16)
    blocks = [t.astype(jnp.bfloat16) for t in tiles] + [parts]
    for p in range(peers):
        for j in range(slots):
            message[p, j] = blocks[j]


def first_kernel(density, moment_map, message):
    n = message.shape[1] - 1
    w = message.shape[3]
    tiles = [density[:, j * w : (j + 1) * w] for j in range(n)]
    emit_message(tiles, moment_map, message)


def moment_kernel(received, out):
    peers, slots = received.shape[:2]
    total = received[0, slots - 1].astype(jnp.float32)
    for p in range(1, peers):
        total = total + received[p, slots - 1].astype(jnp.float32)
    row = jnp.sum(total, axis=0, keepdims=True)
    for g in range(out.shape[0]):
        out[g] = row


def shift_of(power):
    assert power & (power - 1) == 0
    return power.bit_length() - 1


def far_weights(centres, first, reach):
    shape = (reach, centres.shape[1])
    rows = row_ids(shape)
    q = lax.broadcasted_iota(jnp.int32, shape, 1)
    theirs = [jnp.broadcast_to(centres[c : c + 1, :], shape) for c in range(3)]
    mine = [jnp.take_along_axis(t, first + rows, axis=1) for t in theirs]
    d0, d1, d2 = (m - t for m, t in zip(mine, theirs))
    mirrored = mine[2] + theirs[2]
    direct_sq = d0 * d0 + d1 * d1 + d2 * d2
    image_sq = d0 * d0 + d1 * d1 + mirrored * mirrored
    kernel = 1.0 / jnp.sqrt(direct_sq + 1.0) + 1.0 / jnp.sqrt(image_sq + 1.0)
    return jnp.where(jnp.abs(first + rows - q) > reach, kernel, 0.0)


def sweep_kernel(
    colour_now,
    last,
    near_bubble,
    near_block,
    near_count,
    colour,
    centres,
    before,
    own,
    after,
    moments,
    spread_map,
    right_side,
    relaxed,
    moment_map,
    near_vals,
    inv_diag,
    *refs,
):
    if last:
        out, sources, acc = refs
    else:
        out, message, sources, acc = refs
    bub, nblk, slots, blk, _ = near_vals.shape
    peers = own.shape[0]
    k = blk // bub
    none = 3 * peers * nblk * bub
    rows = row_ids((bub, blk))
    for o, ref in enumerate((before, own, after)):
        for p in range(peers):
            for j in range(nblk):
                at = ((o * peers + p) * nblk + j) * bub
                sources[at : at + bub, :] = ref[p, j].astype(jnp.float32)
    sources[none:, :] = jnp.zeros((bub, blk), jnp.float32)
    acc[...] = jnp.zeros_like(acc)

    first = lax.axis_index("bubble") * bub
    weight = far_weights(centres, first, bub)
    lane = lax.broadcasted_iota(jnp.int32, (bub, blk), 1)
    g = jnp.zeros((bub, blk), jnp.float32)
    for q in range(moments.shape[0]):
        g = g + jnp.take_along_axis(weight, q * bub + lane // k, axis=1) * moments[q]
    shift = blk // 2
    while shift >= k:
        g = g + pltpu.roll(g, shift, 1)
        shift //= 2
    coeff = jnp.where(lane // k == rows, g, 0.0).astype(jnp.bfloat16)
    far = lax.dot_general(coeff, spread_map[...], NN, preferred_element_type=jnp.float32)

    def near_of(b, carry):
        @pl.when(colour[b] == colour_now)
        def _():
            here = rows == b
            for r in range(nblk):
                total = acc[r]
                for s in range(slots):
                    local = near_bubble[r, s, b] - (first - bub)
                    row = ((local >> shift_of(bub)) * peers * nblk + near_block[r, s, b]) * bub
                    i = jnp.where(s < near_count[b, r], row + (local & (bub - 1)), none)
                    src = jnp.where(here, sources[pl.ds(i, 1), :], 0.0).astype(jnp.bfloat16)
                    total = total + lax.dot_general(
                        src, near_vals[b, r, s], NT, preferred_element_type=jnp.float32
                    )
                acc[r] = total

        return carry

    lax.fori_loop(0, bub, near_of, 0)
    for r in range(nblk):
        cols = slice(r * blk, (r + 1) * blk)
        acc[r] = right_side[:, cols] - acc[r] - far[:, cols]
        out[:, cols] = jnp.zeros((bub, blk), jnp.float32)

    def solve(b, carry):
        @pl.when(colour[b] == colour_now)
        def _():
            here = rows == b
            for r in range(nblk):
                cols = slice(r * blk, (r + 1) * blk)
                rest = jnp.where(here, acc[r], 0.0).astype(jnp.bfloat16)
                out[:, cols] += lax.dot_general(
                    rest, inv_diag[b, r], NT, preferred_element_type=jnp.float32
                )

        return carry

    lax.fori_loop(0, bub, solve, 0)
    colours = jnp.zeros((bub, blk), jnp.int32)
    for b in range(bub):
        colours = jnp.where(rows == b, colour[b], colours)
    live = colours == colour_now
    tiles = []
    for r in range(nblk):
        cols = slice(r * blk, (r + 1) * blk)
        tile = jnp.where(live, out[:, cols], relaxed[:, cols])
        out[:, cols] = tile
        tiles.append(tile)
    if not last:
        emit_message(tiles, moment_map, message)


VMEM = pl.BlockSpec(memory_space=pltpu.VMEM)
SMEM = pl.BlockSpec(memory_space=pltpu.SMEM)


def limit(mib):
    return pltpu.CompilerParams(vmem_limit_bytes=mib << 20)


def per_device(
    density,
    right_side,
    inv_diag,
    near_vals,
    near_bubble,
    near_block,
    near_count,
    colour,
    moment_map,
    spread_map,
    centres,
):
    bub, nblk, slots, blk, _ = near_vals.shape
    k = moment_map.shape[1]
    panels = nblk * blk
    peers, groups = lax.axis_size("panel"), lax.axis_size("bubble")
    moment_map = moment_map.reshape(bub * k, panels)
    spread_map = spread_map.reshape(bub * k, panels)

    message_shape = jax.ShapeDtypeStruct((peers, nblk + 1, bub, blk), jnp.bfloat16)
    relaxed_shape = jax.ShapeDtypeStruct((bub, panels), jnp.float32)
    up = [(i, (i + 1) % groups) for i in range(groups)]
    down = [(j, i) for i, j in up]

    message = pl.pallas_call(
        first_kernel,
        out_shape=message_shape,
        in_specs=[VMEM, VMEM],
        out_specs=VMEM,
        compiler_params=limit(2),
        cost_estimate=pl.CostEstimate(flops=1 << 34, bytes_accessed=1 << 20, transcendentals=0),
        name="first",
    )(density, moment_map)
    near_bubble = near_bubble.transpose(1, 2, 0)
    near_block = near_block.transpose(1, 2, 0)
    relaxed = density
    for colour_now in range(2):
        last = colour_now == 1
        received = lax.all_to_all(message, "panel", 0, 0, tiled=True)
        before = lax.ppermute(received, "bubble", up)
        after = lax.ppermute(received, "bubble", down)
        own_moments = pl.pallas_call(
            moment_kernel,
            out_shape=jax.ShapeDtypeStruct((groups, 1, blk), jnp.float32),
            in_specs=[VMEM],
            out_specs=VMEM,
            compiler_params=limit(2),
            name="moments",
        )(received)
        moments = lax.all_to_all(own_moments, "bubble", 0, 0, tiled=True)
        outs = pl.pallas_call(
            functools.partial(sweep_kernel, colour_now, last),
            out_shape=[relaxed_shape] if last else [relaxed_shape, message_shape],
            in_specs=[SMEM] * 4 + [VMEM] * 11,
            out_specs=[VMEM] if last else [VMEM, VMEM],
            scratch_shapes=[
                pltpu.VMEM(((3 * peers * nblk + 1) * bub, blk), jnp.float32),
                pltpu.VMEM((nblk, bub, blk), jnp.float32),
            ],
            compiler_params=limit(4),
            name=f"sweep{colour_now}",
        )(
            near_bubble,
            near_block,
            near_count,
            colour,
            centres,
            before,
            received,
            after,
            moments,
            spread_map,
            right_side,
            relaxed,
            moment_map,
            near_vals,
            inv_diag,
        )
        if last:
            (relaxed,) = outs
        else:
            relaxed, message = outs
    return relaxed


def solution(mesh):
    in_specs = (
        P("bubble", "panel"),
        P("bubble", "panel"),
        P("bubble", "panel", None, None),
        P("bubble", "panel", None, None, None),
        P("bubble", "panel", None),
        P("bubble", "panel", None),
        P("bubble", "panel"),
        P("bubble"),
        P("bubble", None, "panel"),
        P("bubble", None, "panel"),
        P(),
    )
    out_specs = P("bubble", "panel")
    return jax.shard_map(
        per_device, mesh=mesh, in_specs=in_specs, out_specs=out_specs, check_vma=False
    )
```

```python
import functools

import jax
import jax.numpy as jnp
from jax import lax
from jax.experimental import pallas as pl
from jax.experimental.pallas import tpu as pltpu
from jax.sharding import PartitionSpec as P


NT = (((1,), (1,)), ((), ()))
NN = (((1,), (0,)), ((), ()))


def row_ids(shape):
    return lax.broadcasted_iota(jnp.int32, shape, 0)


def emit_message(tiles, moment_map, message):
    bub, lanes = tiles[0].shape
    peers, slots = message.shape[:2]
    k = lanes // bub
    dens = jnp.concatenate(tiles, axis=1).astype(jnp.bfloat16)
    cross = lax.dot_general(dens, moment_map[...], NT, preferred_element_type=jnp.float32)
    rows = row_ids((bub, lanes))
    own = lax.broadcasted_iota(jnp.int32, (bub, lanes), 1) // k == rows
    share = jnp.sum(jnp.where(own, cross, 0.0), axis=0, keepdims=True)
    top = share.astype(jnp.bfloat16).astype(jnp.float32)
    rest = share - top
    mid = rest.astype(jnp.bfloat16).astype(jnp.float32)
    low = rest - mid
    parts = jnp.where(
        rows == 0, top, jnp.where(rows == 1, mid, jnp.where(rows == 2, low, 0.0))
    ).astype(jnp.bfloat16)
    blocks = [t.astype(jnp.bfloat16) for t in tiles] + [parts]
    for p in range(peers):
        for j in range(slots):
            message[p, j] = blocks[j]


def first_kernel(density_hbm, map_hbm, message, density, moment_map, sems):
    copies = [
        pltpu.make_async_copy(map_hbm, moment_map, sems.at[0]),
        pltpu.make_async_copy(density_hbm, density, sems.at[1]),
    ]
    for c in copies:
        c.start()
    for c in copies:
        c.wait()
    n = message.shape[1] - 1
    w = message.shape[3]
    tiles = [density[:, j * w : (j + 1) * w] for j in range(n)]
    emit_message(tiles, moment_map, message)


def moment_kernel(received, out):
    peers, slots = received.shape[:2]
    total = received[0, slots - 1].astype(jnp.float32)
    for p in range(1, peers):
        total = total + received[p, slots - 1].astype(jnp.float32)
    row = jnp.sum(total, axis=0, keepdims=True)
    for g in range(out.shape[0]):
        out[g] = row


def shift_of(power):
    assert power & (power - 1) == 0
    return power.bit_length() - 1


def far_weights(centres, first, reach):
    shape = (reach, centres.shape[1])
    rows = row_ids(shape)
    q = lax.broadcasted_iota(jnp.int32, shape, 1)
    theirs = [jnp.broadcast_to(centres[c : c + 1, :], shape) for c in range(3)]
    mine = [jnp.take_along_axis(t, first + rows, axis=1) for t in theirs]
    d0, d1, d2 = (m - t for m, t in zip(mine, theirs))
    mirrored = mine[2] + theirs[2]
    direct_sq = d0 * d0 + d1 * d1 + d2 * d2
    image_sq = d0 * d0 + d1 * d1 + mirrored * mirrored
    kernel = 1.0 / jnp.sqrt(direct_sq + 1.0) + 1.0 / jnp.sqrt(image_sq + 1.0)
    return jnp.where(jnp.abs(first + rows - q) > reach, kernel, 0.0)


def near_kernel(
    colour_now,
    near_bubble,
    near_block,
    near_count,
    colour,
    odd_swap,
    own,
    even_swap,
    near_vals,
    acc,
    sources,
    vals,
    sems,
):
    bub, nblk, slots, blk, _ = near_vals.shape
    peers = own.shape[0]
    my_index = lax.axis_index("bubble")
    first = my_index * bub
    even = (my_index & 1) == 0
    none = 3 * peers * nblk * bub

    def copy(b):
        return pltpu.make_async_copy(near_vals.at[b], vals.at[b], sems.at[b])

    for b in range(bub):

        @pl.when(colour[b] == colour_now)
        def _():
            copy(b).start()

    rows = row_ids((bub, blk))
    for o, ref in enumerate((odd_swap, own, even_swap)):
        for p in range(peers):
            for j in range(nblk):
                at = ((o * peers + p) * nblk + j) * bub
                sources[at : at + bub, :] = ref[p, j].astype(jnp.float32)
    sources[none:, :] = jnp.zeros((bub, blk), jnp.float32)
    acc[...] = jnp.zeros_like(acc)

    def near_of(b, carry):
        @pl.when(colour[b] == colour_now)
        def _():
            copy(b).wait()
            here = rows == b
            for r in range(nblk):
                picked = []
                for s in range(slots):
                    local = near_bubble[r, s, b] - (first - bub)
                    o = local >> shift_of(bub)
                    o = jnp.where(even, o, 2 - o)
                    row = (o * peers * nblk + near_block[r, s, b]) * bub + (local & (bub - 1))
                    i = jnp.where(s < near_count[b, r], row, none)
                    picked.append(jnp.where(here, sources[pl.ds(i, 1), :], 0.0))
                src = jnp.concatenate(picked, axis=1).astype(jnp.bfloat16)
                block = jnp.concatenate([vals[b, r, s] for s in range(slots)], axis=1)
                acc[r] += lax.dot_general(src, block, NT, preferred_element_type=jnp.float32)

        return carry

    lax.fori_loop(0, bub, near_of, 0)


def finish_kernel(
    colour_now,
    last,
    colour,
    centres,
    moments,
    near,
    spread_map,
    right_side,
    relaxed,
    moment_map,
    inv_diag,
    *refs,
):
    bub, nblk, blk, _ = inv_diag.shape
    k = blk // bub
    out = refs[0]
    rows = row_ids((bub, blk))

    first = lax.axis_index("bubble") * bub
    weight = far_weights(centres, first, bub)
    lane = lax.broadcasted_iota(jnp.int32, (bub, blk), 1)
    g = jnp.zeros((bub, blk), jnp.float32)
    for q in range(moments.shape[0]):
        g = g + jnp.take_along_axis(weight, q * bub + lane // k, axis=1) * moments[q]
    shift = blk // 2
    while shift >= k:
        g = g + pltpu.roll(g, shift, 1)
        shift //= 2
    coeff = jnp.where(lane // k == rows, g, 0.0).astype(jnp.bfloat16)
    far = lax.dot_general(coeff, spread_map[...], NN, preferred_element_type=jnp.float32)

    colours = jnp.zeros((bub, blk), jnp.int32)
    for b in range(bub):
        colours = jnp.where(rows == b, colour[b], colours)
    live = colours == colour_now
    tiles = []
    for r in range(nblk):
        cols = slice(r * blk, (r + 1) * blk)
        rest = right_side[:, cols] - near[r] - far[:, cols]
        rest = jnp.where(live, rest, 0.0)
        updated = jnp.zeros((bub, blk), jnp.float32)
        for b in range(0, bub, 2):
            pair = jnp.concatenate(
                [jnp.where(rows == b, rest, 0.0), jnp.where(rows == b + 1, rest, 0.0)], axis=1
            ).astype(jnp.bfloat16)
            block = jnp.concatenate([inv_diag[b, r], inv_diag[b + 1, r]], axis=1)
            updated = updated + lax.dot_general(
                pair, block, NT, preferred_element_type=jnp.float32
            )
        tile = jnp.where(live, updated, relaxed[:, cols])
        out[:, cols] = tile
        tiles.append(tile)
    if not last:
        emit_message(tiles, moment_map, refs[1])


VMEM = pl.BlockSpec(memory_space=pltpu.VMEM)
SMEM = pl.BlockSpec(memory_space=pltpu.SMEM)
HBM = pl.BlockSpec(memory_space=pltpu.HBM)


def in_hbm(x):
    return pltpu.with_memory_space_constraint(x, pltpu.HBM)


def limit(mib):
    return pltpu.CompilerParams(vmem_limit_bytes=mib << 20)


def per_device(
    density,
    right_side,
    inv_diag,
    near_vals,
    near_bubble,
    near_block,
    near_count,
    colour,
    moment_map,
    spread_map,
    centres,
):
    bub, nblk, slots, blk, _ = near_vals.shape
    k = moment_map.shape[1]
    panels = nblk * blk
    peers, groups = lax.axis_size("panel"), lax.axis_size("bubble")
    moment_map = moment_map.reshape(bub * k, panels)
    spread_map = spread_map.reshape(bub * k, panels)

    message_shape = jax.ShapeDtypeStruct((peers, nblk + 1, bub, blk), jnp.bfloat16)
    relaxed_shape = jax.ShapeDtypeStruct((bub, panels), jnp.float32)
    pairs = [(i, i + 1) for i in range(groups - 1)]
    odd_pairs = [(i, j) for p in pairs[1::2] for i, j in (p, p[::-1])]
    even_pairs = [(i, j) for p in pairs[0::2] for i, j in (p, p[::-1])]

    message = pl.pallas_call(
        first_kernel,
        out_shape=message_shape,
        in_specs=[HBM, HBM],
        out_specs=VMEM,
        scratch_shapes=[
            pltpu.VMEM((bub, panels), jnp.float32),
            pltpu.VMEM((bub * k, panels), jnp.bfloat16),
            pltpu.SemaphoreType.DMA((2,)),
        ],
        compiler_params=limit(2),
        cost_estimate=pl.CostEstimate(flops=1 << 34, bytes_accessed=1 << 20, transcendentals=0),
        name="first",
    )(in_hbm(density), in_hbm(moment_map))
    near_vals = in_hbm(near_vals)
    near_bubble = near_bubble.transpose(1, 2, 0)
    near_block = near_block.transpose(1, 2, 0)
    relaxed = density
    for colour_now in range(2):
        last = colour_now == 1
        received = lax.all_to_all(message, "panel", 0, 0, tiled=True)
        odd_swap = lax.ppermute(received, "bubble", odd_pairs)
        even_swap = lax.ppermute(received, "bubble", even_pairs)
        own_moments = pl.pallas_call(
            moment_kernel,
            out_shape=jax.ShapeDtypeStruct((groups, 1, blk), jnp.float32),
            in_specs=[VMEM],
            out_specs=VMEM,
            compiler_params=limit(2),
            name="moments",
        )(received)
        moments = lax.all_to_all(own_moments, "bubble", 0, 0, tiled=True)
        near = pl.pallas_call(
            functools.partial(near_kernel, colour_now),
            out_shape=jax.ShapeDtypeStruct((nblk, bub, blk), jnp.float32),
            in_specs=[SMEM] * 4 + [VMEM] * 3 + [HBM],
            out_specs=VMEM,
            scratch_shapes=[
                pltpu.VMEM(((3 * peers * nblk + 1) * bub, blk), jnp.float32),
                pltpu.VMEM((bub, nblk, slots, blk, blk), jnp.bfloat16),
                pltpu.SemaphoreType.DMA((bub,)),
            ],
            compiler_params=limit(12),
        )(near_bubble, near_block, near_count, colour, odd_swap, received, even_swap, near_vals)
        outs = pl.pallas_call(
            functools.partial(finish_kernel, colour_now, last),
            out_shape=[relaxed_shape] if last else [relaxed_shape, message_shape],
            in_specs=[SMEM] + [VMEM] * 8,
            out_specs=[VMEM] if last else [VMEM, VMEM],
            compiler_params=limit(4),
        )(colour, centres, moments, near, spread_map, right_side, relaxed, moment_map, inv_diag)
        if last:
            (relaxed,) = outs
        else:
            relaxed, message = outs
    return relaxed


def solution(mesh):
    in_specs = (
        P("bubble", "panel"),
        P("bubble", "panel"),
        P("bubble", "panel", None, None),
        P("bubble", "panel", None, None, None),
        P("bubble", "panel", None),
        P("bubble", "panel", None),
        P("bubble", "panel"),
        P("bubble"),
        P("bubble", None, "panel"),
        P("bubble", None, "panel"),
        P(),
    )
    out_specs = P("bubble", "panel")

    return jax.shard_map(
        per_device, mesh=mesh, in_specs=in_specs, out_specs=out_specs, check_vma=False
    )
```

```python
import functools

import jax
import jax.numpy as jnp
from jax import lax
from jax.experimental import pallas as pl
from jax.experimental.pallas import tpu as pltpu
from jax.sharding import PartitionSpec as P


NT = (((1,), (1,)), ((), ()))
NN = (((1,), (0,)), ((), ()))


def row_ids(shape):
    return lax.broadcasted_iota(jnp.int32, shape, 0)


def emit_message(tiles, moment_map, message):
    bub, lanes = tiles[0].shape
    peers, slots = message.shape[:2]
    k = lanes // bub
    dens = jnp.concatenate(tiles, axis=1).astype(jnp.bfloat16)
    cross = lax.dot_general(dens, moment_map[...], NT, preferred_element_type=jnp.float32)
    rows = row_ids((bub, lanes))
    own = lax.broadcasted_iota(jnp.int32, (bub, lanes), 1) // k == rows
    share = jnp.sum(jnp.where(own, cross, 0.0), axis=0, keepdims=True)
    top = share.astype(jnp.bfloat16).astype(jnp.float32)
    rest = share - top
    mid = rest.astype(jnp.bfloat16).astype(jnp.float32)
    low = rest - mid
    parts = jnp.where(
        rows == 0, top, jnp.where(rows == 1, mid, jnp.where(rows == 2, low, 0.0))
    ).astype(jnp.bfloat16)
    blocks = [t.astype(jnp.bfloat16) for t in tiles] + [parts]
    for p in range(peers):
        for j in range(slots):
            message[p, j] = blocks[j]


def first_kernel(density_hbm, map_hbm, message, density, moment_map, sems):
    copies = [
        pltpu.make_async_copy(map_hbm, moment_map, sems.at[0]),
        pltpu.make_async_copy(density_hbm, density, sems.at[1]),
    ]
    for c in copies:
        c.start()
    for c in copies:
        c.wait()
    n = message.shape[1] - 1
    w = message.shape[3]
    tiles = [density[:, j * w : (j + 1) * w] for j in range(n)]
    emit_message(tiles, moment_map, message)


def moment_kernel(received, out):
    peers, slots = received.shape[:2]
    total = received[0, slots - 1].astype(jnp.float32)
    for p in range(1, peers):
        total = total + received[p, slots - 1].astype(jnp.float32)
    row = jnp.sum(total, axis=0, keepdims=True)
    for g in range(out.shape[0]):
        out[g] = row


def shift_of(power):
    assert power & (power - 1) == 0
    return power.bit_length() - 1


def far_weights(centres, first, reach):
    shape = (reach, centres.shape[1])
    rows = row_ids(shape)
    q = lax.broadcasted_iota(jnp.int32, shape, 1)
    theirs = [jnp.broadcast_to(centres[c : c + 1, :], shape) for c in range(3)]
    mine = [jnp.take_along_axis(t, first + rows, axis=1) for t in theirs]
    d0, d1, d2 = (m - t for m, t in zip(mine, theirs))
    mirrored = mine[2] + theirs[2]
    direct_sq = d0 * d0 + d1 * d1 + d2 * d2
    image_sq = d0 * d0 + d1 * d1 + mirrored * mirrored
    kernel = 1.0 / jnp.sqrt(direct_sq + 1.0) + 1.0 / jnp.sqrt(image_sq + 1.0)
    return jnp.where(jnp.abs(first + rows - q) > reach, kernel, 0.0)


def near_kernel(
    colour_now,
    near_bubble,
    near_block,
    near_count,
    colour,
    centres,
    odd_swap,
    own,
    even_swap,
    right_side,
    near_vals,
    rest,
    live,
    *refs,
):
    *weights, sources, vals, sems = refs
    bub, nblk, slots, blk, _ = near_vals.shape
    peers = own.shape[0]
    my_index = lax.axis_index("bubble")
    first = my_index * bub
    even = (my_index & 1) == 0
    none = 3 * peers * nblk * bub

    def copy(b):
        return pltpu.make_async_copy(near_vals.at[b], vals.at[b], sems.at[b])

    for b in range(bub):

        @pl.when(colour[b] == colour_now)
        def _():
            copy(b).start()

    rows = row_ids((bub, blk))
    for o, ref in enumerate((odd_swap, own, even_swap)):
        for p in range(peers):
            for j in range(nblk):
                at = ((o * peers + p) * nblk + j) * bub
                sources[at : at + bub, :] = ref[p, j].astype(jnp.float32)
    sources[none:, :] = jnp.zeros((bub, blk), jnp.float32)
    colours = jnp.zeros((bub, blk), jnp.int32)
    for b in range(bub):
        colours = jnp.where(rows == b, colour[b], colours)
    live[...] = (colours == colour_now).astype(jnp.float32)
    for r in range(nblk):
        rest[r] = right_side[:, r * blk : (r + 1) * blk]
    for table in weights:
        weight = far_weights(centres, first, bub)
        lane = lax.broadcasted_iota(jnp.int32, (bub, blk), 1)
        for q in range(table.shape[0]):
            table[q] = jnp.take_along_axis(weight, q * bub + lane // (blk // bub), axis=1)

    def near_of(b, carry):
        @pl.when(colour[b] == colour_now)
        def _():
            copy(b).wait()
            here = rows == b
            for r in range(nblk):
                picked = []
                for s in range(slots):
                    local = near_bubble[r, s, b] - (first - bub)
                    o = local >> shift_of(bub)
                    o = jnp.where(even, o, 2 - o)
                    row = (o * peers * nblk + near_block[r, s, b]) * bub + (local & (bub - 1))
                    i = jnp.where(s < near_count[b, r], row, none)
                    picked.append(jnp.where(here, sources[pl.ds(i, 1), :], 0.0))
                src = jnp.concatenate(picked, axis=1).astype(jnp.bfloat16)
                block = jnp.concatenate([vals[b, r, s] for s in range(slots)], axis=1)
                rest[r] -= lax.dot_general(src, block, NT, preferred_element_type=jnp.float32)

        return carry

    lax.fori_loop(0, bub, near_of, 0)


def finish_kernel(
    last,
    moments,
    weights,
    rest,
    live,
    spread_map,
    relaxed,
    moment_map,
    inv_diag,
    *refs,
):
    bub, nblk, blk, _ = inv_diag.shape
    k = blk // bub
    out = refs[0]
    rows = row_ids((bub, blk))
    lane = lax.broadcasted_iota(jnp.int32, (bub, blk), 1)

    terms = [weights[q] * moments[q] for q in range(moments.shape[0])]
    while len(terms) > 1:
        terms = [u + v for u, v in zip(terms[::2], terms[1::2])]
    g = terms[0]
    shift = blk // 2
    while shift >= k:
        g = g + pltpu.roll(g, shift, 1)
        shift //= 2
    coeff = jnp.where(lane // k == rows, g, 0.0).astype(jnp.bfloat16)
    far = lax.dot_general(coeff, spread_map[...], NN, preferred_element_type=jnp.float32)

    is_live = live[...] > 0.5
    tiles = []
    for r in range(nblk):
        cols = slice(r * blk, (r + 1) * blk)
        remainder = rest[r] - far[:, cols]
        updated = jnp.zeros((bub, blk), jnp.float32)
        for b in range(0, bub, 2):
            pair = jnp.concatenate(
                [jnp.where(rows == b + h, remainder, 0.0) for h in range(2)], axis=1
            ).astype(jnp.bfloat16)
            block = jnp.concatenate([inv_diag[b, r], inv_diag[b + 1, r]], axis=1)
            updated = updated + lax.dot_general(
                pair, block, NT, preferred_element_type=jnp.float32
            )
        tile = jnp.where(is_live, updated, relaxed[:, cols])
        out[:, cols] = tile
        tiles.append(tile)
    if not last:
        emit_message(tiles, moment_map, refs[1])


VMEM = pl.BlockSpec(memory_space=pltpu.VMEM)
SMEM = pl.BlockSpec(memory_space=pltpu.SMEM)
HBM = pl.BlockSpec(memory_space=pltpu.HBM)


def in_hbm(x):
    return pltpu.with_memory_space_constraint(x, pltpu.HBM)


def limit(mib):
    return pltpu.CompilerParams(vmem_limit_bytes=mib << 20)


def per_device(
    density,
    right_side,
    inv_diag,
    near_vals,
    near_bubble,
    near_block,
    near_count,
    colour,
    moment_map,
    spread_map,
    centres,
):
    bub, nblk, slots, blk, _ = near_vals.shape
    k = moment_map.shape[1]
    panels = nblk * blk
    peers, groups = lax.axis_size("panel"), lax.axis_size("bubble")
    moment_map = moment_map.reshape(bub * k, panels)
    spread_map = spread_map.reshape(bub * k, panels)

    message_shape = jax.ShapeDtypeStruct((peers, nblk + 1, bub, blk), jnp.bfloat16)
    near_shapes = [
        jax.ShapeDtypeStruct((nblk, bub, blk), jnp.float32),
        jax.ShapeDtypeStruct((bub, blk), jnp.float32),
        jax.ShapeDtypeStruct((groups, bub, blk), jnp.float32),
    ]
    relaxed_shape = jax.ShapeDtypeStruct((bub, panels), jnp.float32)
    pairs = [(i, i + 1) for i in range(groups - 1)]
    odd_pairs = [(i, j) for p in pairs[1::2] for i, j in (p, p[::-1])]
    odd_pairs += [(0, groups - 1), (groups - 1, 0)]
    even_pairs = [(i, j) for p in pairs[0::2] for i, j in (p, p[::-1])]

    message = pl.pallas_call(
        first_kernel,
        out_shape=message_shape,
        in_specs=[HBM, HBM],
        out_specs=VMEM,
        scratch_shapes=[
            pltpu.VMEM((bub, panels), jnp.float32),
            pltpu.VMEM((bub * k, panels), jnp.bfloat16),
            pltpu.SemaphoreType.DMA((2,)),
        ],
        compiler_params=limit(2),
        cost_estimate=pl.CostEstimate(flops=1 << 34, bytes_accessed=1 << 20, transcendentals=0),
        name="first",
    )(in_hbm(density), in_hbm(moment_map))
    near_vals = in_hbm(near_vals)
    near_bubble = near_bubble.transpose(1, 2, 0)
    near_block = near_block.transpose(1, 2, 0)
    relaxed = density
    for colour_now in range(2):
        last = colour_now == 1
        received = lax.all_to_all(message, "panel", 0, 0, tiled=True)
        even_swap = lax.ppermute(received, "bubble", even_pairs)
        odd_swap = lax.ppermute(received, "bubble", odd_pairs)
        own_moments = pl.pallas_call(
            moment_kernel,
            out_shape=jax.ShapeDtypeStruct((groups, 1, blk), jnp.float32),
            in_specs=[VMEM],
            out_specs=VMEM,
            compiler_params=limit(2),
            name="moments",
        )(received)
        moments = lax.all_to_all(own_moments, "bubble", 0, 0, tiled=True)
        rest, live, *table = pl.pallas_call(
            functools.partial(near_kernel, colour_now),
            out_shape=near_shapes[: 2 if last else 3],
            in_specs=[SMEM] * 4 + [VMEM] * 5 + [HBM],
            out_specs=[VMEM] * (2 if last else 3),
            scratch_shapes=[
                pltpu.VMEM(((3 * peers * nblk + 1) * bub, blk), jnp.float32),
                pltpu.VMEM((bub, nblk, slots, blk, blk), jnp.bfloat16),
                pltpu.SemaphoreType.DMA((bub,)),
            ],
            compiler_params=limit(12),
        )(
            near_bubble,
            near_block,
            near_count,
            colour,
            centres,
            odd_swap,
            received,
            even_swap,
            right_side,
            near_vals,
        )
        weights = table[0] if table else weights
        outs = pl.pallas_call(
            functools.partial(finish_kernel, last),
            out_shape=[relaxed_shape] if last else [relaxed_shape, message_shape],
            in_specs=[VMEM] * 8,
            out_specs=[VMEM] if last else [VMEM, VMEM],
            compiler_params=limit(4),
        )(moments, weights, rest, live, spread_map, relaxed, moment_map, inv_diag)
        if last:
            (relaxed,) = outs
        else:
            relaxed, message = outs
    return relaxed


def solution(mesh):
    in_specs = (
        P("bubble", "panel"),
        P("bubble", "panel"),
        P("bubble", "panel", None, None),
        P("bubble", "panel", None, None, None),
        P("bubble", "panel", None),
        P("bubble", "panel", None),
        P("bubble", "panel"),
        P("bubble"),
        P("bubble", None, "panel"),
        P("bubble", None, "panel"),
        P(),
    )
    out_specs = P("bubble", "panel")

    return jax.shard_map(
        per_device, mesh=mesh, in_specs=in_specs, out_specs=out_specs, check_vma=False
    )
```

```python
import functools

import jax
import jax.numpy as jnp
from jax import lax
from jax.experimental import pallas as pl
from jax.experimental.pallas import tpu as pltpu
from jax.sharding import PartitionSpec as P


NT = (((1,), (1,)), ((), ()))
NN = (((1,), (0,)), ((), ()))


def row_ids(shape):
    return lax.broadcasted_iota(jnp.int32, shape, 0)


def emit_message(tiles, moment_map, message):
    bub, lanes = tiles[0].shape
    peers, slots = message.shape[:2]
    k = lanes // bub
    dens = jnp.concatenate(tiles, axis=1).astype(jnp.bfloat16)
    cross = lax.dot_general(dens, moment_map[...], NT, preferred_element_type=jnp.float32)
    rows = row_ids((bub, lanes))
    own = lax.broadcasted_iota(jnp.int32, (bub, lanes), 1) // k == rows
    share = jnp.sum(jnp.where(own, cross, 0.0), axis=0, keepdims=True)
    top = share.astype(jnp.bfloat16).astype(jnp.float32)
    rest = share - top
    mid = rest.astype(jnp.bfloat16).astype(jnp.float32)
    low = rest - mid
    parts = jnp.where(
        rows == 0, top, jnp.where(rows == 1, mid, jnp.where(rows == 2, low, 0.0))
    ).astype(jnp.bfloat16)
    blocks = [t.astype(jnp.bfloat16) for t in tiles] + [parts]
    for p in range(peers):
        for j in range(slots):
            message[p, j] = blocks[j]


def first_kernel(density_hbm, map_hbm, message, density, moment_map, sems):
    copies = [
        pltpu.make_async_copy(map_hbm, moment_map, sems.at[0]),
        pltpu.make_async_copy(density_hbm, density, sems.at[1]),
    ]
    for c in copies:
        c.start()
    for c in copies:
        c.wait()
    n = message.shape[1] - 1
    w = message.shape[3]
    tiles = [density[:, j * w : (j + 1) * w] for j in range(n)]
    emit_message(tiles, moment_map, message)


def moment_kernel(received, out):
    peers, slots = received.shape[:2]
    total = received[0, slots - 1].astype(jnp.float32)
    for p in range(1, peers):
        total = total + received[p, slots - 1].astype(jnp.float32)
    row = jnp.sum(total, axis=0, keepdims=True)
    for g in range(out.shape[0]):
        out[g] = row


def shift_of(power):
    assert power & (power - 1) == 0
    return power.bit_length() - 1


def far_weights(centres, first, reach):
    shape = (reach, centres.shape[1])
    rows = row_ids(shape)
    q = lax.broadcasted_iota(jnp.int32, shape, 1)
    theirs = [jnp.broadcast_to(centres[c : c + 1, :], shape) for c in range(3)]
    mine = [jnp.take_along_axis(t, first + rows, axis=1) for t in theirs]
    d0, d1, d2 = (m - t for m, t in zip(mine, theirs))
    mirrored = mine[2] + theirs[2]
    direct_sq = d0 * d0 + d1 * d1 + d2 * d2
    image_sq = d0 * d0 + d1 * d1 + mirrored * mirrored
    kernel = 1.0 / jnp.sqrt(direct_sq + 1.0) + 1.0 / jnp.sqrt(image_sq + 1.0)
    return jnp.where(jnp.abs(first + rows - q) > reach, kernel, 0.0)


def near_kernel(
    colour_now,
    near_bubble,
    near_block,
    near_count,
    colour,
    centres,
    fetched,
    own,
    traded,
    right_side,
    near_vals,
    rest,
    live,
    *refs,
):
    *weights, sources, vals, sems = refs
    bub, nblk, slots, blk, _ = near_vals.shape
    peers = own.shape[0]
    my_index = lax.axis_index("bubble")
    first = my_index * bub
    in_order = (my_index & 1) == (lax.axis_index("panel") & 1) ^ 1
    none = 3 * peers * nblk * bub

    def copy(b):
        return pltpu.make_async_copy(near_vals.at[b], vals.at[b], sems.at[b])

    for b in range(bub):

        @pl.when(colour[b] == colour_now)
        def _():
            copy(b).start()

    rows = row_ids((bub, blk))
    for o, ref in enumerate((fetched, own, traded)):
        for p in range(peers):
            for j in range(nblk):
                at = ((o * peers + p) * nblk + j) * bub
                sources[at : at + bub, :] = ref[p, j].astype(jnp.float32)
    sources[none:, :] = jnp.zeros((bub, blk), jnp.float32)
    colours = jnp.zeros((bub, blk), jnp.int32)
    for b in range(bub):
        colours = jnp.where(rows == b, colour[b], colours)
    live[...] = (colours == colour_now).astype(jnp.float32)
    for r in range(nblk):
        rest[r] = right_side[:, r * blk : (r + 1) * blk]
    for table in weights:
        weight = far_weights(centres, first, bub)
        lane = lax.broadcasted_iota(jnp.int32, (bub, blk), 1)
        for q in range(table.shape[0]):
            table[q] = jnp.take_along_axis(weight, q * bub + lane // (blk // bub), axis=1)

    def near_of(b, carry):
        @pl.when(colour[b] == colour_now)
        def _():
            copy(b).wait()
            here = rows == b
            for r in range(nblk):
                picked = []
                for s in range(slots):
                    local = near_bubble[r, s, b] - (first - bub)
                    o = local >> shift_of(bub)
                    o = jnp.where(in_order, o, 2 - o)
                    row = (o * peers * nblk + near_block[r, s, b]) * bub + (local & (bub - 1))
                    i = jnp.where(s < near_count[b, r], row, none)
                    picked.append(jnp.where(here, sources[pl.ds(i, 1), :], 0.0))
                src = jnp.concatenate(picked, axis=1).astype(jnp.bfloat16)
                block = jnp.concatenate([vals[b, r, s] for s in range(slots)], axis=1)
                rest[r] -= lax.dot_general(src, block, NT, preferred_element_type=jnp.float32)

        return carry

    lax.fori_loop(0, bub, near_of, 0)


def finish_kernel(
    last,
    moments,
    weights,
    rest,
    live,
    spread_map,
    relaxed,
    moment_map,
    inv_diag,
    *refs,
):
    bub, nblk, blk, _ = inv_diag.shape
    k = blk // bub
    out = refs[0]
    rows = row_ids((bub, blk))
    lane = lax.broadcasted_iota(jnp.int32, (bub, blk), 1)

    terms = [weights[q] * moments[q] for q in range(moments.shape[0])]
    while len(terms) > 1:
        terms = [u + v for u, v in zip(terms[::2], terms[1::2])]
    g = terms[0]
    shift = blk // 2
    while shift >= k:
        g = g + pltpu.roll(g, shift, 1)
        shift //= 2
    coeff = jnp.where(lane // k == rows, g, 0.0).astype(jnp.bfloat16)
    far = lax.dot_general(coeff, spread_map[...], NN, preferred_element_type=jnp.float32)

    is_live = live[...] > 0.5
    tiles = []
    for r in range(nblk):
        cols = slice(r * blk, (r + 1) * blk)
        remainder = rest[r] - far[:, cols]
        updated = jnp.zeros((bub, blk), jnp.float32)
        for b in range(0, bub, 2):
            pair = jnp.concatenate(
                [jnp.where(rows == b + h, remainder, 0.0) for h in range(2)], axis=1
            ).astype(jnp.bfloat16)
            block = jnp.concatenate([inv_diag[b, r], inv_diag[b + 1, r]], axis=1)
            updated = updated + lax.dot_general(
                pair, block, NT, preferred_element_type=jnp.float32
            )
        tile = jnp.where(is_live, updated, relaxed[:, cols])
        out[:, cols] = tile
        tiles.append(tile)
    if not last:
        emit_message(tiles, moment_map, refs[1])


VMEM = pl.BlockSpec(memory_space=pltpu.VMEM)
SMEM = pl.BlockSpec(memory_space=pltpu.SMEM)
HBM = pl.BlockSpec(memory_space=pltpu.HBM)


def in_hbm(x):
    return pltpu.with_memory_space_constraint(x, pltpu.HBM)


def limit(mib):
    return pltpu.CompilerParams(vmem_limit_bytes=mib << 20)


def per_device(
    density,
    right_side,
    inv_diag,
    near_vals,
    near_bubble,
    near_block,
    near_count,
    colour,
    moment_map,
    spread_map,
    centres,
):
    bub, nblk, slots, blk, _ = near_vals.shape
    k = moment_map.shape[1]
    panels = nblk * blk
    peers, groups = lax.axis_size("panel"), lax.axis_size("bubble")
    moment_map = moment_map.reshape(bub * k, panels)
    spread_map = spread_map.reshape(bub * k, panels)

    message_shape = jax.ShapeDtypeStruct((peers, nblk + 1, bub, blk), jnp.bfloat16)
    near_shapes = [
        jax.ShapeDtypeStruct((nblk, bub, blk), jnp.float32),
        jax.ShapeDtypeStruct((bub, blk), jnp.float32),
        jax.ShapeDtypeStruct((groups, bub, blk), jnp.float32),
    ]
    relaxed_shape = jax.ShapeDtypeStruct((bub, panels), jnp.float32)
    fetch = []
    for g in range(groups):
        for p in range(peers):
            other = g ^ 1 if p % 2 == 0 else ((g + 1) ^ 1) - 1
            fetch.append((g * peers + p, other % groups * peers + p))
    trade = [(p, p ^ 1) for p in range(peers)]

    message = pl.pallas_call(
        first_kernel,
        out_shape=message_shape,
        in_specs=[HBM, HBM],
        out_specs=VMEM,
        scratch_shapes=[
            pltpu.VMEM((bub, panels), jnp.float32),
            pltpu.VMEM((bub * k, panels), jnp.bfloat16),
            pltpu.SemaphoreType.DMA((2,)),
        ],
        compiler_params=limit(2),
        cost_estimate=pl.CostEstimate(flops=1 << 34, bytes_accessed=1 << 20, transcendentals=0),
        name="first",
    )(in_hbm(density), in_hbm(moment_map))
    near_vals = in_hbm(near_vals)
    near_bubble = near_bubble.transpose(1, 2, 0)
    near_block = near_block.transpose(1, 2, 0)
    relaxed = density
    for colour_now in range(2):
        last = colour_now == 1
        received = lax.all_to_all(message, "panel", 0, 0, tiled=True)
        fetched = lax.ppermute(received, ("bubble", "panel"), fetch)
        traded = lax.ppermute(fetched, "panel", trade)
        own_moments = pl.pallas_call(
            moment_kernel,
            out_shape=jax.ShapeDtypeStruct((groups, 1, blk), jnp.float32),
            in_specs=[VMEM],
            out_specs=VMEM,
            compiler_params=limit(2),
            name="moments",
        )(received)
        moments = lax.all_to_all(own_moments, "bubble", 0, 0, tiled=True)
        rest, live, *table = pl.pallas_call(
            functools.partial(near_kernel, colour_now),
            out_shape=near_shapes[: 2 if last else 3],
            in_specs=[SMEM] * 4 + [VMEM] * 5 + [HBM],
            out_specs=[VMEM] * (2 if last else 3),
            scratch_shapes=[
                pltpu.VMEM(((3 * peers * nblk + 1) * bub, blk), jnp.float32),
                pltpu.VMEM((bub, nblk, slots, blk, blk), jnp.bfloat16),
                pltpu.SemaphoreType.DMA((bub,)),
            ],
            compiler_params=limit(12),
        )(
            near_bubble,
            near_block,
            near_count,
            colour,
            centres,
            fetched,
            received,
            traded,
            right_side,
            near_vals,
        )
        weights = table[0] if table else weights
        outs = pl.pallas_call(
            functools.partial(finish_kernel, last),
            out_shape=[relaxed_shape] if last else [relaxed_shape, message_shape],
            in_specs=[VMEM] * 8,
            out_specs=[VMEM] if last else [VMEM, VMEM],
            compiler_params=limit(4),
        )(moments, weights, rest, live, spread_map, relaxed, moment_map, inv_diag)
        if last:
            (relaxed,) = outs
        else:
            relaxed, message = outs
    return relaxed


def solution(mesh):
    in_specs = (
        P("bubble", "panel"),
        P("bubble", "panel"),
        P("bubble", "panel", None, None),
        P("bubble", "panel", None, None, None),
        P("bubble", "panel", None),
        P("bubble", "panel", None),
        P("bubble", "panel"),
        P("bubble"),
        P("bubble", None, "panel"),
        P("bubble", None, "panel"),
        P(),
    )
    out_specs = P("bubble", "panel")

    return jax.shard_map(
        per_device, mesh=mesh, in_specs=in_specs, out_specs=out_specs, check_vma=False
    )
```

```python
import functools

import jax
import jax.numpy as jnp
from jax import lax
from jax.experimental import pallas as pl
from jax.experimental.pallas import tpu as pltpu
from jax.sharding import PartitionSpec as P


NT = (((1,), (1,)), ((), ()))
NN = (((1,), (0,)), ((), ()))


def row_ids(shape):
    return lax.broadcasted_iota(jnp.int32, shape, 0)


def emit_message(tiles, moment_map, message):
    bub, lanes = tiles[0].shape
    peers, slots = message.shape[:2]
    k = lanes // bub
    dens = jnp.concatenate(tiles, axis=1).astype(jnp.bfloat16)
    cross = lax.dot_general(dens, moment_map[...], NT, preferred_element_type=jnp.float32)
    rows = row_ids((bub, lanes))
    own = lax.broadcasted_iota(jnp.int32, (bub, lanes), 1) // k == rows
    share = jnp.sum(jnp.where(own, cross, 0.0), axis=0, keepdims=True)
    top = share.astype(jnp.bfloat16).astype(jnp.float32)
    rest = share - top
    mid = rest.astype(jnp.bfloat16).astype(jnp.float32)
    low = rest - mid
    parts = jnp.where(
        rows == 0, top, jnp.where(rows == 1, mid, jnp.where(rows == 2, low, 0.0))
    ).astype(jnp.bfloat16)
    blocks = [t.astype(jnp.bfloat16) for t in tiles] + [parts]
    for p in range(peers):
        for j in range(slots):
            message[p, j] = blocks[j]


def first_kernel(density_hbm, map_hbm, message, density, moment_map, sems):
    copies = [
        pltpu.make_async_copy(map_hbm, moment_map, sems.at[0]),
        pltpu.make_async_copy(density_hbm, density, sems.at[1]),
    ]
    for c in copies:
        c.start()
    for c in copies:
        c.wait()
    n = message.shape[1] - 1
    w = message.shape[3]
    tiles = [density[:, j * w : (j + 1) * w] for j in range(n)]
    emit_message(tiles, moment_map, message)


def moment_kernel(received, out):
    peers, slots = received.shape[:2]
    total = received[0, slots - 1].astype(jnp.float32)
    for p in range(1, peers):
        total = total + received[p, slots - 1].astype(jnp.float32)
    row = jnp.sum(total, axis=0, keepdims=True)
    for g in range(out.shape[0]):
        out[g] = row


def shift_of(power):
    assert power & (power - 1) == 0
    return power.bit_length() - 1


def far_weights(centres, first, reach):
    shape = (reach, centres.shape[1])
    rows = row_ids(shape)
    q = lax.broadcasted_iota(jnp.int32, shape, 1)
    theirs = [jnp.broadcast_to(centres[c : c + 1, :], shape) for c in range(3)]
    mine = [jnp.take_along_axis(t, first + rows, axis=1) for t in theirs]
    d0, d1, d2 = (m - t for m, t in zip(mine, theirs))
    mirrored = mine[2] + theirs[2]
    direct_sq = d0 * d0 + d1 * d1 + d2 * d2
    image_sq = d0 * d0 + d1 * d1 + mirrored * mirrored
    kernel = 1.0 / jnp.sqrt(direct_sq + 1.0) + 1.0 / jnp.sqrt(image_sq + 1.0)
    return jnp.where(jnp.abs(first + rows - q) > reach, kernel, 0.0)


def near_kernel(
    colour_now,
    near_bubble_in,
    near_block_in,
    near_count_in,
    colour_in,
    centres,
    fetched,
    own,
    traded,
    right_side,
    near_vals,
    rest,
    live,
    *refs,
):
    *weights, sources, vals, near_bubble, near_block, near_count, colour, table_sems, sems = refs
    tables = [
        pltpu.make_async_copy(src, dst, table_sems.at[n])
        for n, (src, dst) in enumerate(
            (
                (colour_in, colour),
                (near_bubble_in, near_bubble),
                (near_block_in, near_block),
                (near_count_in, near_count),
            )
        )
    ]
    for t in tables:
        t.start()
    tables[0].wait()
    bub, nblk, slots, blk, _ = near_vals.shape
    peers = own.shape[0]
    my_index = lax.axis_index("bubble")
    first = my_index * bub
    in_order = (my_index & 1) == (lax.axis_index("panel") & 1) ^ 1
    none = 3 * peers * nblk * bub

    def copy(b):
        return pltpu.make_async_copy(near_vals.at[b], vals.at[b], sems.at[b])

    for b in range(bub):

        @pl.when(colour[b] == colour_now)
        def _():
            copy(b).start()

    rows = row_ids((bub, blk))
    for o, ref in enumerate((fetched, own, traded)):
        for p in range(peers):
            for j in range(nblk):
                at = ((o * peers + p) * nblk + j) * bub
                sources[at : at + bub, :] = ref[p, j].astype(jnp.float32)
    sources[none:, :] = jnp.zeros((bub, blk), jnp.float32)
    colours = jnp.zeros((bub, blk), jnp.int32)
    for b in range(bub):
        colours = jnp.where(rows == b, colour[b], colours)
    live[...] = (colours == colour_now).astype(jnp.float32)
    for r in range(nblk):
        rest[r] = right_side[:, r * blk : (r + 1) * blk]
    for table in weights:
        weight = far_weights(centres, first, bub)
        lane = lax.broadcasted_iota(jnp.int32, (bub, blk), 1)
        for q in range(table.shape[0]):
            table[q] = jnp.take_along_axis(weight, q * bub + lane // (blk // bub), axis=1)

    for t in tables[1:]:
        t.wait()

    def near_of(b, carry):
        @pl.when(colour[b] == colour_now)
        def _():
            copy(b).wait()
            here = rows == b
            for r in range(nblk):
                picked = []
                for s in range(slots):
                    local = near_bubble[r, s, b] - (first - bub)
                    o = local >> shift_of(bub)
                    o = jnp.where(in_order, o, 2 - o)
                    row = (o * peers * nblk + near_block[r, s, b]) * bub + (local & (bub - 1))
                    i = jnp.where(s < near_count[b, r], row, none)
                    picked.append(jnp.where(here, sources[pl.ds(i, 1), :], 0.0))
                src = jnp.concatenate(picked, axis=1).astype(jnp.bfloat16)
                block = jnp.concatenate([vals[b, r, s] for s in range(slots)], axis=1)
                rest[r] -= lax.dot_general(src, block, NT, preferred_element_type=jnp.float32)

        return carry

    lax.fori_loop(0, bub, near_of, 0)


def finish_kernel(
    last,
    moments,
    weights,
    rest,
    live,
    spread_map,
    relaxed,
    moment_map,
    inv_diag,
    *refs,
):
    bub, nblk, blk, _ = inv_diag.shape
    k = blk // bub
    out = refs[0]
    rows = row_ids((bub, blk))
    lane = lax.broadcasted_iota(jnp.int32, (bub, blk), 1)

    terms = [weights[q] * moments[q] for q in range(moments.shape[0])]
    while len(terms) > 1:
        terms = [u + v for u, v in zip(terms[::2], terms[1::2])]
    g = terms[0]
    shift = blk // 2
    while shift >= k:
        g = g + pltpu.roll(g, shift, 1)
        shift //= 2
    coeff = jnp.where(lane // k == rows, g, 0.0).astype(jnp.bfloat16)
    far = lax.dot_general(coeff, spread_map[...], NN, preferred_element_type=jnp.float32)

    is_live = live[...] > 0.5
    tiles = []
    for r in range(nblk):
        cols = slice(r * blk, (r + 1) * blk)
        remainder = rest[r] - far[:, cols]
        updated = jnp.zeros((bub, blk), jnp.float32)
        for b in range(0, bub, 2):
            pair = jnp.concatenate(
                [jnp.where(rows == b + h, remainder, 0.0) for h in range(2)], axis=1
            ).astype(jnp.bfloat16)
            block = jnp.concatenate([inv_diag[b, r], inv_diag[b + 1, r]], axis=1)
            updated = updated + lax.dot_general(
                pair, block, NT, preferred_element_type=jnp.float32
            )
        tile = jnp.where(is_live, updated, relaxed[:, cols])
        out[:, cols] = tile
        tiles.append(tile)
    if not last:
        emit_message(tiles, moment_map, refs[1])


VMEM = pl.BlockSpec(memory_space=pltpu.VMEM)
SMEM = pl.BlockSpec(memory_space=pltpu.SMEM)
HBM = pl.BlockSpec(memory_space=pltpu.HBM)


def in_hbm(x):
    return pltpu.with_memory_space_constraint(x, pltpu.HBM)


def limit(mib):
    return pltpu.CompilerParams(vmem_limit_bytes=mib << 20)


def per_device(
    density,
    right_side,
    inv_diag,
    near_vals,
    near_bubble,
    near_block,
    near_count,
    colour,
    moment_map,
    spread_map,
    centres,
):
    bub, nblk, slots, blk, _ = near_vals.shape
    k = moment_map.shape[1]
    panels = nblk * blk
    peers, groups = lax.axis_size("panel"), lax.axis_size("bubble")
    moment_map = moment_map.reshape(bub * k, panels)
    spread_map = spread_map.reshape(bub * k, panels)

    message_shape = jax.ShapeDtypeStruct((peers, nblk + 1, bub, blk), jnp.bfloat16)
    near_shapes = [
        jax.ShapeDtypeStruct((nblk, bub, blk), jnp.float32),
        jax.ShapeDtypeStruct((bub, blk), jnp.float32),
        jax.ShapeDtypeStruct((groups, bub, blk), jnp.float32),
    ]
    relaxed_shape = jax.ShapeDtypeStruct((bub, panels), jnp.float32)
    fetch = []
    for g in range(groups):
        for p in range(peers):
            other = g ^ 1 if p % 2 == 0 else ((g + 1) ^ 1) - 1
            if 0 <= other < groups:
                fetch.append((g * peers + p, other * peers + p))
            else:
                fetch.append((g * peers + p, g * peers + (p ^ 2)))
    trade = [(p, p ^ 1) for p in range(peers)]

    message = pl.pallas_call(
        first_kernel,
        out_shape=message_shape,
        in_specs=[HBM, HBM],
        out_specs=VMEM,
        scratch_shapes=[
            pltpu.VMEM((bub, panels), jnp.float32),
            pltpu.VMEM((bub * k, panels), jnp.bfloat16),
            pltpu.SemaphoreType.DMA((2,)),
        ],
        compiler_params=limit(2),
        cost_estimate=pl.CostEstimate(flops=1 << 34, bytes_accessed=1 << 20, transcendentals=0),
        name="first",
    )(in_hbm(density), in_hbm(moment_map))
    near_vals = in_hbm(near_vals)
    near_bubble = near_bubble.transpose(1, 2, 0)
    near_block = near_block.transpose(1, 2, 0)
    relaxed = density
    for colour_now in range(2):
        last = colour_now == 1
        received = lax.all_to_all(message, "panel", 0, 0, tiled=True)
        fetched = lax.ppermute(received, ("bubble", "panel"), fetch)
        traded = lax.ppermute(fetched, "panel", trade)
        own_moments = pl.pallas_call(
            moment_kernel,
            out_shape=jax.ShapeDtypeStruct((groups, 1, blk), jnp.float32),
            in_specs=[VMEM],
            out_specs=VMEM,
            compiler_params=limit(2),
            name="moments",
        )(received)
        moments = lax.all_to_all(own_moments, "bubble", 0, 0, tiled=True)
        rest, live, *table = pl.pallas_call(
            functools.partial(near_kernel, colour_now),
            out_shape=near_shapes[: 2 if last else 3],
            in_specs=[VMEM] * 9 + [HBM],
            out_specs=[VMEM] * (2 if last else 3),
            scratch_shapes=[
                pltpu.VMEM(((3 * peers * nblk + 1) * bub, blk), jnp.float32),
                pltpu.VMEM((bub, nblk, slots, blk, blk), jnp.bfloat16),
                pltpu.SMEM((nblk, slots, bub), jnp.int32),
                pltpu.SMEM((nblk, slots, bub), jnp.int32),
                pltpu.SMEM((bub, nblk), jnp.int32),
                pltpu.SMEM((bub,), jnp.int32),
                pltpu.SemaphoreType.DMA((4,)),
                pltpu.SemaphoreType.DMA((bub,)),
            ],
            compiler_params=limit(12),
        )(
            near_bubble,
            near_block,
            near_count,
            colour,
            centres,
            fetched,
            received,
            traded,
            right_side,
            near_vals,
        )
        weights = table[0] if table else weights
        outs = pl.pallas_call(
            functools.partial(finish_kernel, last),
            out_shape=[relaxed_shape] if last else [relaxed_shape, message_shape],
            in_specs=[VMEM] * 8,
            out_specs=[VMEM] if last else [VMEM, VMEM],
            compiler_params=limit(4),
        )(moments, weights, rest, live, spread_map, relaxed, moment_map, inv_diag)
        if last:
            (relaxed,) = outs
        else:
            relaxed, message = outs
    return relaxed


def solution(mesh):
    in_specs = (
        P("bubble", "panel"),
        P("bubble", "panel"),
        P("bubble", "panel", None, None),
        P("bubble", "panel", None, None, None),
        P("bubble", "panel", None),
        P("bubble", "panel", None),
        P("bubble", "panel"),
        P("bubble"),
        P("bubble", None, "panel"),
        P("bubble", None, "panel"),
        P(),
    )
    out_specs = P("bubble", "panel")

    return jax.shard_map(
        per_device, mesh=mesh, in_specs=in_specs, out_specs=out_specs, check_vma=False
    )
```

```python
import functools

import jax
import jax.numpy as jnp
from jax import lax
from jax.experimental import pallas as pl
from jax.experimental.pallas import tpu as pltpu
from jax.sharding import PartitionSpec as P


NT = (((1,), (1,)), ((), ()))
NN = (((1,), (0,)), ((), ()))


def row_ids(shape):
    return lax.broadcasted_iota(jnp.int32, shape, 0)


def emit_message(tiles, moment_map, message):
    bub, lanes = tiles[0].shape
    peers, slots = message.shape[:2]
    k = lanes // bub
    dens = jnp.concatenate(tiles, axis=1).astype(jnp.bfloat16)
    cross = lax.dot_general(dens, moment_map[...], NT, preferred_element_type=jnp.float32)
    rows = row_ids((bub, lanes))
    own = lax.broadcasted_iota(jnp.int32, (bub, lanes), 1) // k == rows
    share = jnp.sum(jnp.where(own, cross, 0.0), axis=0, keepdims=True)
    top = share.astype(jnp.bfloat16).astype(jnp.float32)
    rest = share - top
    mid = rest.astype(jnp.bfloat16).astype(jnp.float32)
    low = rest - mid
    parts = jnp.where(
        rows == 0, top, jnp.where(rows == 1, mid, jnp.where(rows == 2, low, 0.0))
    ).astype(jnp.bfloat16)
    blocks = [t.astype(jnp.bfloat16) for t in tiles] + [parts]
    for p in range(peers):
        for j in range(slots):
            message[p, j] = blocks[j]


def first_kernel(density_hbm, map_hbm, message, density, moment_map, sems):
    copies = [
        pltpu.make_async_copy(map_hbm, moment_map, sems.at[0]),
        pltpu.make_async_copy(density_hbm, density, sems.at[1]),
    ]
    for c in copies:
        c.start()
    for c in copies:
        c.wait()
    n = message.shape[1] - 1
    w = message.shape[3]
    tiles = [density[:, j * w : (j + 1) * w] for j in range(n)]
    emit_message(tiles, moment_map, message)


def moment_kernel(received, out):
    peers, slots = received.shape[:2]
    total = received[0, slots - 1].astype(jnp.float32)
    for p in range(1, peers):
        total = total + received[p, slots - 1].astype(jnp.float32)
    row = jnp.sum(total, axis=0, keepdims=True)
    for g in range(out.shape[0]):
        out[g] = row


def shift_of(power):
    assert power & (power - 1) == 0
    return power.bit_length() - 1


def far_weights(centres, first, reach):
    shape = (reach, centres.shape[1])
    rows = row_ids(shape)
    q = lax.broadcasted_iota(jnp.int32, shape, 1)
    theirs = [jnp.broadcast_to(centres[c : c + 1, :], shape) for c in range(3)]
    mine = [jnp.take_along_axis(t, first + rows, axis=1) for t in theirs]
    d0, d1, d2 = (m - t for m, t in zip(mine, theirs))
    mirrored = mine[2] + theirs[2]
    direct_sq = d0 * d0 + d1 * d1 + d2 * d2
    image_sq = d0 * d0 + d1 * d1 + mirrored * mirrored
    kernel = 1.0 / jnp.sqrt(direct_sq + 1.0) + 1.0 / jnp.sqrt(image_sq + 1.0)
    return jnp.where(jnp.abs(first + rows - q) > reach, kernel, 0.0)


def near_kernel(
    colour_now,
    near_bubble_in,
    near_block_in,
    near_count_in,
    colour_in,
    centres,
    fetched,
    own,
    traded,
    right_side,
    near_vals,
    rest,
    live,
    *refs,
):
    *weights, sources, vals, near_bubble, near_block, near_count, colour, table_sems, sems = refs
    tables = [
        pltpu.make_async_copy(src, dst, table_sems.at[n])
        for n, (src, dst) in enumerate(
            (
                (colour_in, colour),
                (near_bubble_in, near_bubble),
                (near_block_in, near_block),
                (near_count_in, near_count),
            )
        )
    ]
    for t in tables:
        t.start()
    tables[0].wait()
    bub, nblk, slots, blk, _ = near_vals.shape
    peers = own.shape[0]
    my_index = lax.axis_index("bubble")
    first = my_index * bub
    in_order = (my_index & 1) == (lax.axis_index("panel") & 1) ^ 1
    none = 3 * peers * nblk * bub

    def copy(b):
        return pltpu.make_async_copy(near_vals.at[b], vals.at[b], sems.at[b])

    for b in range(bub):

        @pl.when(colour[b] == colour_now)
        def _():
            copy(b).start()

    rows = row_ids((bub, blk))
    for o, ref in enumerate((fetched, own, traded)):
        for p in range(peers):
            for j in range(nblk):
                at = ((o * peers + p) * nblk + j) * bub
                sources[at : at + bub, :] = ref[p, j].astype(jnp.float32)
    sources[none:, :] = jnp.zeros((bub, blk), jnp.float32)
    colours = jnp.zeros((bub, blk), jnp.int32)
    for b in range(bub):
        colours = jnp.where(rows == b, colour[b], colours)
    live[...] = (colours == colour_now).astype(jnp.float32)
    for r in range(nblk):
        rest[r] = right_side[:, r * blk : (r + 1) * blk]
    for table in weights:
        weight = far_weights(centres, first, bub)
        lane = lax.broadcasted_iota(jnp.int32, (bub, blk), 1)
        for q in range(table.shape[0]):
            table[q] = jnp.take_along_axis(weight, q * bub + lane // (blk // bub), axis=1)

    for t in tables[1:]:
        t.wait()

    def near_of(b, carry):
        @pl.when(colour[b] == colour_now)
        def _():
            copy(b).wait()
            here = rows == b
            for r in range(nblk):
                picked = []
                for s in range(slots):
                    local = near_bubble[r, s, b] - (first - bub)
                    o = local >> shift_of(bub)
                    o = jnp.where(in_order, o, 2 - o)
                    row = (o * peers * nblk + near_block[r, s, b]) * bub + (local & (bub - 1))
                    i = jnp.where(s < near_count[b, r], row, none)
                    picked.append(jnp.where(here, sources[pl.ds(i, 1), :], 0.0))
                src = jnp.concatenate(picked, axis=1).astype(jnp.bfloat16)
                block = jnp.concatenate([vals[b, r, s] for s in range(slots)], axis=1)
                rest[r] -= lax.dot_general(src, block, NT, preferred_element_type=jnp.float32)

        return carry

    lax.fori_loop(0, bub, near_of, 0)


def finish_kernel(
    last,
    moments,
    weights,
    rest,
    live,
    spread_map,
    relaxed,
    moment_map,
    inv_diag,
    *refs,
):
    bub, nblk, blk, _ = inv_diag.shape
    k = blk // bub
    out = refs[0]
    rows = row_ids((bub, blk))
    lane = lax.broadcasted_iota(jnp.int32, (bub, blk), 1)

    terms = [weights[q] * moments[q] for q in range(moments.shape[0])]
    while len(terms) > 1:
        terms = [u + v for u, v in zip(terms[::2], terms[1::2])]
    g = terms[0]
    shift = blk // 2
    while shift >= k:
        g = g + pltpu.roll(g, shift, 1)
        shift //= 2
    coeff = jnp.where(lane // k == rows, g, 0.0).astype(jnp.bfloat16)
    far = lax.dot_general(coeff, spread_map[...], NN, preferred_element_type=jnp.float32)

    is_live = live[...] > 0.5
    tiles = []
    for r in range(nblk):
        cols = slice(r * blk, (r + 1) * blk)
        remainder = rest[r] - far[:, cols]
        updated = jnp.zeros((bub, blk), jnp.float32)
        for b in range(0, bub, 4):
            pair = jnp.concatenate(
                [jnp.where(rows == b + h, remainder, 0.0) for h in range(4)], axis=1
            ).astype(jnp.bfloat16)
            block = jnp.concatenate([inv_diag[b + h, r] for h in range(4)], axis=1)
            updated = updated + lax.dot_general(
                pair, block, NT, preferred_element_type=jnp.float32
            )
        tile = jnp.where(is_live, updated, relaxed[:, cols])
        out[:, cols] = tile
        tiles.append(tile)
    if not last:
        emit_message(tiles, moment_map, refs[1])


VMEM = pl.BlockSpec(memory_space=pltpu.VMEM)
SMEM = pl.BlockSpec(memory_space=pltpu.SMEM)
HBM = pl.BlockSpec(memory_space=pltpu.HBM)


def in_hbm(x):
    return pltpu.with_memory_space_constraint(x, pltpu.HBM)


def limit(mib):
    return pltpu.CompilerParams(vmem_limit_bytes=mib << 20)


def per_device(
    density,
    right_side,
    inv_diag,
    near_vals,
    near_bubble,
    near_block,
    near_count,
    colour,
    moment_map,
    spread_map,
    centres,
):
    bub, nblk, slots, blk, _ = near_vals.shape
    k = moment_map.shape[1]
    panels = nblk * blk
    peers, groups = lax.axis_size("panel"), lax.axis_size("bubble")
    moment_map = moment_map.reshape(bub * k, panels)
    spread_map = spread_map.reshape(bub * k, panels)

    message_shape = jax.ShapeDtypeStruct((peers, nblk + 1, bub, blk), jnp.bfloat16)
    near_shapes = [
        jax.ShapeDtypeStruct((nblk, bub, blk), jnp.float32),
        jax.ShapeDtypeStruct((bub, blk), jnp.float32),
        jax.ShapeDtypeStruct((groups, bub, blk), jnp.float32),
    ]
    relaxed_shape = jax.ShapeDtypeStruct((bub, panels), jnp.float32)
    fetch = []
    for g in range(groups):
        for p in range(peers):
            other = g ^ 1 if p % 2 == 0 else ((g + 1) ^ 1) - 1
            if 0 <= other < groups:
                fetch.append((g * peers + p, other * peers + p))
            else:
                fetch.append((g * peers + p, g * peers + (p ^ 2)))
    trade = [(p, p ^ 1) for p in range(peers)]

    message = pl.pallas_call(
        first_kernel,
        out_shape=message_shape,
        in_specs=[HBM, HBM],
        out_specs=VMEM,
        scratch_shapes=[
            pltpu.VMEM((bub, panels), jnp.float32),
            pltpu.VMEM((bub * k, panels), jnp.bfloat16),
            pltpu.SemaphoreType.DMA((2,)),
        ],
        compiler_params=limit(2),
        cost_estimate=pl.CostEstimate(flops=1 << 34, bytes_accessed=1 << 20, transcendentals=0),
        name="first",
    )(in_hbm(density), in_hbm(moment_map))
    near_vals = in_hbm(near_vals)
    near_bubble = near_bubble.transpose(1, 2, 0)
    near_block = near_block.transpose(1, 2, 0)
    relaxed = density
    for colour_now in range(2):
        last = colour_now == 1
        received = lax.all_to_all(message, "panel", 0, 0, tiled=True)
        fetched = lax.ppermute(received, ("bubble", "panel"), fetch)
        traded = lax.ppermute(fetched, "panel", trade)
        own_moments = pl.pallas_call(
            moment_kernel,
            out_shape=jax.ShapeDtypeStruct((groups, 1, blk), jnp.float32),
            in_specs=[VMEM],
            out_specs=VMEM,
            compiler_params=limit(2),
            name="moments",
        )(received)
        moments = lax.all_to_all(own_moments, "bubble", 0, 0, tiled=True)
        rest, live, *table = pl.pallas_call(
            functools.partial(near_kernel, colour_now),
            out_shape=near_shapes[: 2 if last else 3],
            in_specs=[VMEM] * 9 + [HBM],
            out_specs=[VMEM] * (2 if last else 3),
            scratch_shapes=[
                pltpu.VMEM(((3 * peers * nblk + 1) * bub, blk), jnp.float32),
                pltpu.VMEM((bub, nblk, slots, blk, blk), jnp.bfloat16),
                pltpu.SMEM((nblk, slots, bub), jnp.int32),
                pltpu.SMEM((nblk, slots, bub), jnp.int32),
                pltpu.SMEM((bub, nblk), jnp.int32),
                pltpu.SMEM((bub,), jnp.int32),
                pltpu.SemaphoreType.DMA((4,)),
                pltpu.SemaphoreType.DMA((bub,)),
            ],
            compiler_params=limit(12),
        )(
            near_bubble,
            near_block,
            near_count,
            colour,
            centres,
            fetched,
            received,
            traded,
            right_side,
            near_vals,
        )
        weights = table[0] if table else weights
        outs = pl.pallas_call(
            functools.partial(finish_kernel, last),
            out_shape=[relaxed_shape] if last else [relaxed_shape, message_shape],
            in_specs=[VMEM] * 8,
            out_specs=[VMEM] if last else [VMEM, VMEM],
            compiler_params=limit(4),
        )(moments, weights, rest, live, spread_map, relaxed, moment_map, inv_diag)
        if last:
            (relaxed,) = outs
        else:
            relaxed, message = outs
    return relaxed


def solution(mesh):
    in_specs = (
        P("bubble", "panel"),
        P("bubble", "panel"),
        P("bubble", "panel", None, None),
        P("bubble", "panel", None, None, None),
        P("bubble", "panel", None),
        P("bubble", "panel", None),
        P("bubble", "panel"),
        P("bubble"),
        P("bubble", None, "panel"),
        P("bubble", None, "panel"),
        P(),
    )
    out_specs = P("bubble", "panel")

    return jax.shard_map(
        per_device, mesh=mesh, in_specs=in_specs, out_specs=out_specs, check_vma=False
    )
```
